256 devices in a mesh: blk: 16 (over x_lo, y, core), rep: 16 (over z, x_hi).
Axes of the slice: x: 4 (x_hi: 2, x_lo: 2; x = x_hi * 2 + x_lo), y: 4, z: 8, core: 2. Of those that a mesh axis runs over, the one named last changes fastest.
Arguments:
- stale: bfloat16 [32768, 512], P(('blk', 'rep')), may hold values from -6 to 6
- w_self: bfloat16 [512, 512], replicated, may hold values from -0.25 to 0.25
- w_neigh: bfloat16 [512, 512], replicated, may hold values from -6 to 6
- tile_weights: bfloat16 [16, 16, 16, 12, 128, 128], P('blk', 'rep'), may hold values from 0 to 4, as said below
- tile_pos: int32 [16, 16, 16, 12], P('blk', 'rep'), may hold values from 0 to 15, as said below
- tile_counts: int32 [16, 16, 16], P('blk', 'rep'), may hold values from 0 to 12, as said below
Outputs:
- refreshed: bfloat16 [32768, 512], P(('blk', 'rep'))
The draws below stay inside these ranges and needn't reach their ends.
Inputs may be any that keep to these rules, and one draw needn't show every extreme that they name: `tile_weights`: non-negative edge weights. `tile_pos`: distinct within the live head of every list. `tile_counts`: every device has one full list.
All inputs are finite; a program needn't handle non-finite values.
Results may differ from the reference program's by a relative error of at most 0.013.
Values may be sent and summed in bfloat16 or wider, within the bound.
No kernel may reach another device: no remote copies, remote signals or barrier semaphores. Data moves between devices by JAX's collectives and lax.ppermute only.
A program may use at most 64 MiB of HBM per device.

```python
import jax
import jax.numpy as jnp
from jax import lax

D = 512
TILE = 128
SB = 128
GROUPS = 16
MEMBERS = 16
CAP = 12
NODES = 32768
N_BLK = 16
N_REP = 16


def draw_tile_weights(key, part):
    first_key, second_key = jax.random.split(key)
    tile_shape = (GROUPS, MEMBERS, GROUPS, CAP, TILE, TILE)
    present = jax.random.uniform(first_key, tile_shape, jnp.float32) < 0.25
    strength = jnp.exp(jax.random.uniform(second_key, tile_shape, jnp.float32, jnp.log(0.25), jnp.log(4.0)))
    return jnp.where(present, strength, 0.0).astype(jnp.bfloat16)


def draw_tile_pos(key, part):
    pair_count = SB * MEMBERS // TILE * (SB // TILE)
    sub_keys = jax.random.split(key, GROUPS * MEMBERS * GROUPS)
    orders = jax.vmap(lambda sub_key: jax.random.permutation(sub_key, pair_count)[:CAP])(sub_keys)
    return orders.reshape(GROUPS, MEMBERS, GROUPS, CAP).astype(jnp.int32)


def draw_tile_counts(key, part):
    first_key, second_key = jax.random.split(key)
    counts = jax.random.randint(first_key, (GROUPS, MEMBERS, GROUPS), 0, CAP + 1, dtype=jnp.int32)
    full_shard = jax.random.randint(second_key, (GROUPS, MEMBERS, 1), 0, GROUPS, dtype=jnp.int32)
    return jnp.where(jnp.arange(GROUPS, dtype=jnp.int32)[None, None, :] == full_shard, CAP, counts).astype(jnp.int32)


def levels(stream_key, extent, pieces, least, largest):
    level, own = 1.0, jax.random.fold_in(stream_key, 6)
    for dim, blocks in pieces:
        heights = jnp.exp(jax.random.uniform(jax.random.fold_in(own, dim), (blocks,), jnp.float32, least / len(pieces), largest / len(pieces)))
        level = level * jnp.repeat(heights, extent[dim] // blocks).reshape([-1 if axis == dim else 1 for axis in range(len(extent))])
    return level


def scatter_about(own_key, shape, scale, most, cuts=(), held_as=jnp.bfloat16):
    values = jax.random.normal(own_key, shape, jnp.float32) * scale
    if len(cuts) > 0:
        values = levels(own_key, shape, cuts, -0.22, 0.18) * values
    return jnp.clip(values, min=-most, max=most).astype(held_as)


def setup_inputs(seed: int = 0) -> dict:
    key_list = jax.random.split(jax.random.key(seed), 7)
    stale = scatter_about(key_list[0], (NODES, D), 1.0, 6.0, ((0, 256),))
    w_self = scatter_about(key_list[1], (D, D), D ** -0.5, 0.25)
    w_neigh = scatter_about(key_list[2], (D, D), (max(1, D * 8 // (N_BLK * N_REP * TILE))) ** -0.5, 6.0)
    tile_weights = draw_tile_weights(jax.random.fold_in(key_list[6], 71), 0)
    tile_pos = draw_tile_pos(jax.random.fold_in(key_list[6], 71), 0)
    tile_counts = draw_tile_counts(jax.random.fold_in(key_list[6], 71), 0)
    return dict(stale=stale, w_self=w_self, w_neigh=w_neigh, tile_weights=tile_weights, tile_pos=tile_pos, tile_counts=tile_counts)


def member_partial(sources, weights, places, counts):
    col_tiles = SB // TILE
    row_tiles = SB * MEMBERS // TILE

    def shard_step(running, inputs):
        totals, degree = running
        source_block, shard_tiles, shard_places, live_count = inputs
        live_mask = (jnp.arange(CAP) < live_count).astype(jnp.float32)
        tiles = shard_tiles.astype(jnp.float32) * live_mask[:, None, None]
        column = shard_places % col_tiles
        row_tile = shard_places // col_tiles
        picked = jnp.take(source_block.reshape(col_tiles, TILE, D), column, axis=0).astype(jnp.float32)
        products = jnp.einsum('kij,kjd->kid', tiles, picked, precision=lax.Precision.HIGHEST)
        onehot = (row_tile[None, :] == jnp.arange(row_tiles)[:, None]).astype(jnp.float32)
        totals = totals + jnp.dot(onehot, products.reshape(CAP, TILE * D), precision=lax.Precision.HIGHEST).reshape(row_tiles * TILE, D)
        degree = degree + jnp.dot(onehot, lax.optimization_barrier(jnp.sum(tiles, axis=2)), precision=lax.Precision.HIGHEST).reshape(row_tiles * TILE)
        return ((totals, degree), None)
    start = (jnp.zeros((SB * MEMBERS, D), jnp.float32), jnp.zeros((SB * MEMBERS,), jnp.float32))
    result, _ = lax.scan(shard_step, start, (sources, weights, places, counts))
    return result

def rounded(values):
    return lax.optimization_barrier(values.astype(jnp.bfloat16)).astype(jnp.float32)

def reference(stale, w_self, w_neigh, tile_weights, tile_pos, tile_counts):
    stale_view = stale.reshape(GROUPS, MEMBERS, SB, D)

    def group_step(unused, group_id):

        def member_step(running, member):
            sources = stale_view[:, member]
            part_sum, part_deg = member_partial(sources, tile_weights[group_id, member], tile_pos[group_id, member], tile_counts[group_id, member])
            return ((running[0] + rounded(part_sum), running[1] + rounded(part_deg)), None)
        start = (jnp.zeros((SB * MEMBERS, D), jnp.float32), jnp.zeros((SB * MEMBERS,), jnp.float32))
        (totals, degree), _ = lax.scan(member_step, start, jnp.arange(MEMBERS))
        own_rows = stale_view[group_id].reshape(SB * MEMBERS, D)
        neighbour_mean = ((own_rows.astype(jnp.float32) + totals) / (1.0 + degree)[:, None]).astype(jnp.bfloat16)
        hidden = jnp.dot(own_rows, w_self, preferred_element_type=jnp.float32) + jnp.dot(neighbour_mean, w_neigh, preferred_element_type=jnp.float32)
        active_out = jnp.maximum(hidden, 0.0)
        refreshed = active_out * lax.rsqrt(lax.optimization_barrier(jnp.mean(active_out * active_out, axis=-1, keepdims=True)) + 1e-05)
        return (unused, refreshed.astype(jnp.bfloat16))
    _, outputs = lax.scan(group_step, jnp.zeros((), jnp.float32), jnp.arange(GROUPS))
    return outputs.reshape(GROUPS * MEMBERS * SB, D)
```

```python
import jax
import jax.numpy as jnp
from jax import lax
from jax.experimental import pallas as pl
from jax.experimental.pallas import tpu as pltpu
from jax.sharding import PartitionSpec as P

NCH = 2
TILE = 128


def rep_at(index, dz, dx):
    z, x = index // 2, index % 2
    return ((z + dz) % 8) * 2 + (x + dx) % 2


def to_rep(value, dz, dx):
    return lax.ppermute(value, "rep", [(i, rep_at(i, dz, dx)) for i in range(16)])


def slot_source(slot, blk):
    return (slot % 8) * 2 + (blk + slot // 8) % 2


def place_kernel(meta, counts, pos, tiles_ref, a_ref, deg_ref, sums):
    slot = pl.program_id(0)
    source = slot_source(slot, meta[0])
    rep = meta[1]
    my_z, my_x = rep // 2, rep % 2

    @pl.when(slot == 0)
    def _():
        sums[...] = jnp.zeros_like(sums)

    a_ref[...] = jnp.zeros_like(a_ref)

    def put(k, carry):
        place = pos[source * tiles_ref.shape[1] + k]
        row = ((place // 2 + 8 - my_z) % 8) * 2 + (place % 2 + my_x) % 2
        tile = tiles_ref[0, k]
        a_ref[0, pl.ds(pl.multiple_of(row * TILE, TILE), TILE), :] = tile
        sums[row] = sums[row] + tile.astype(jnp.float32)
        return carry

    lax.fori_loop(0, counts[source], put, 0)

    @pl.when(slot == pl.num_programs(0) - 1)
    def _():
        mine = lax.broadcasted_iota(jnp.int32, deg_ref.shape[1:], 0) == my_z
        for row in range(deg_ref.shape[0]):
            total = jnp.sum(sums[row].T, axis=0, keepdims=True)
            spread = jnp.broadcast_to(total, deg_ref.shape[1:])
            deg_ref[row] = jnp.where(mine, spread, 0.0).astype(deg_ref.dtype)


def place_tiles(meta, counts, pos, tiles):
    lists, cap = tiles.shape[:2]
    return pl.pallas_call(
        place_kernel,
        grid_spec=pltpu.PrefetchScalarGridSpec(
            num_scalar_prefetch=3,
            grid=(16,),
            in_specs=[
                pl.BlockSpec(
                    (1, cap, TILE, TILE),
                    lambda j, meta, counts, pos: (slot_source(j, meta[0]), 0, 0, 0),
                )
            ],
            out_specs=[
                pl.BlockSpec((1, 2048, TILE), lambda j, *_: (j, 0, 0)),
                pl.BlockSpec((16, 16, TILE), lambda j, *_: (0, 0, 0)),
            ],
            scratch_shapes=[pltpu.VMEM((16, TILE, TILE), jnp.float32)],
        ),
        out_shape=[
            jax.ShapeDtypeStruct((16, 2048, TILE), jnp.bfloat16),
            jax.ShapeDtypeStruct((16, 16, TILE), jnp.bfloat16),
        ],
        compiler_params=pltpu.CompilerParams(vmem_limit_bytes=8 << 20),
        cost_estimate=pl.CostEstimate(flops=4 << 20, transcendentals=0, bytes_accessed=14 << 20),
        name="place_tiles",
    )(meta, counts, pos, pltpu.with_memory_space_constraint(tiles, pltpu.HBM))


def sum_kernel(a_ref, near_ref, far_ref, *refs):
    out_ref = refs[-1]
    half = a_ref.shape[0] // 2
    result = jnp.zeros((2 * TILE, out_ref.shape[-1]), jnp.float32)
    for side, source in enumerate((near_ref, far_ref)):
        left = jnp.concatenate([a_ref[side * half + j] for j in range(half)], axis=1)
        result += jnp.dot(left, source[...], preferred_element_type=jnp.float32)
    result = result.astype(out_ref.dtype)
    out_ref[0, 0, :TILE, :] = result[:TILE]
    out_ref[0, 1, :TILE, :] = result[TILE:]
    if len(refs) > 1:
        deg = refs[0][...]
        out_ref[0, :, TILE:, :] = jnp.concatenate(
            [deg] + [jnp.zeros_like(deg)] * (out_ref.shape[-1] // TILE - 1), axis=2
        )


def partial_sums(a, near, far, degrees=None):
    count, width = far.shape
    rows = TILE
    extra, specs = [], []
    if degrees is not None:
        rows += degrees.shape[1]
        extra = [degrees]
        specs = [pl.BlockSpec((2,) + degrees.shape[1:], lambda i: (i, 0, 0))]
    return pl.pallas_call(
        sum_kernel,
        grid=(8,),
        in_specs=[
            pl.BlockSpec((16, 2 * TILE, TILE), lambda i: (0, i, 0)),
            pl.BlockSpec((count, width), lambda i: (0, 0)),
            pl.BlockSpec((count, width), lambda i: (0, 0)),
        ]
        + specs,
        out_specs=pl.BlockSpec((1, 2, rows, width), lambda i: (i, 0, 0, 0)),
        out_shape=jax.ShapeDtypeStruct((8, 2, rows, width), jnp.bfloat16),
        compiler_params=pltpu.CompilerParams(vmem_limit_bytes=16 << 20),
        cost_estimate=pl.CostEstimate(
            flops=2 * 2048 * 2048 * width, transcendentals=0, bytes_accessed=12 << 20
        ),
        name="partial_sums",
    )(a, near, far, *extra)


def finish_kernel(stale_ref, w_self_ref, w_neigh_ref, *refs):
    out_ref = refs[-1]
    own, other = refs[:NCH], refs[NCH : 2 * NCH]
    stale = stale_ref[...]
    summed = jnp.concatenate(
        [o[:TILE] + r[:TILE].astype(jnp.float32) for o, r in zip(own, other)], axis=1
    )
    degree = jnp.sum(own[0][TILE:, :TILE], axis=0, keepdims=True) + jnp.sum(
        other[0][TILE:, :TILE].astype(jnp.float32), axis=0, keepdims=True
    )
    degree = jnp.broadcast_to(degree, (TILE, TILE)).T
    degree = jnp.concatenate([degree] * (stale.shape[1] // TILE), axis=1)
    mean = ((stale.astype(jnp.float32) + summed) / (1.0 + degree)).astype(jnp.bfloat16)
    hidden = jnp.dot(stale, w_self_ref[...], preferred_element_type=jnp.float32) + jnp.dot(
        mean, w_neigh_ref[...], preferred_element_type=jnp.float32
    )
    active = jnp.maximum(hidden, 0.0)
    out = active * lax.rsqrt(jnp.mean(active * active, axis=-1, keepdims=True) + 1e-05)
    out_ref[...] = out.astype(out_ref.dtype)


def finish(stale, w_self, w_neigh, own, other):
    return pl.pallas_call(
        finish_kernel,
        out_shape=jax.ShapeDtypeStruct(stale.shape, jnp.bfloat16),
        compiler_params=pltpu.CompilerParams(vmem_limit_bytes=8 << 20),
        name="finish",
    )(stale, w_self, w_neigh, *own, *other)


def gather_chunk(part):
    groups = [[i for i in range(16) if i % 2 == c] for c in range(2)]
    spread = jnp.broadcast_to(part, (8,) + part.shape)
    near = lax.all_to_all(spread, "blk", 0, 0, tiled=True, axis_index_groups=groups)
    near = near.reshape(-1, part.shape[-1])
    far = lax.ppermute(near, "blk", [(i, i ^ 1) for i in range(16)])
    return near, far


def scatter_chunk(sums):
    up = to_rep(sums[4, 0:1], 1, 0)
    down = to_rep(sums[4, 1:2], -1, 0)
    up_next = jnp.concatenate([sums[3, 0:1] + up, sums[3, 1:2]], axis=0)
    down_next = jnp.concatenate([sums[5, 0:1], sums[5, 1:2] + down], axis=0)
    up = to_rep(up_next, 1, 0)
    down = to_rep(down_next, -1, 0)
    for step in range(2):
        up = to_rep(sums[2 - step] + up, 1, 0)
        down = to_rep(sums[6 + step] + down, -1, 0)
    total = sums[0].astype(jnp.float32) + up.astype(jnp.float32) + down.astype(jnp.float32)
    other = to_rep(total[1].astype(jnp.bfloat16), 0, 1)
    return total[0], other


def on_device(stale, w_self, w_neigh, tile_weights, tile_pos, tile_counts):
    meta = jnp.stack([lax.axis_index("blk"), lax.axis_index("rep")]).astype(jnp.int32)
    a, degrees = place_tiles(
        meta, tile_counts.reshape(-1), tile_pos.reshape(-1), tile_weights[0, 0]
    )
    width = stale.shape[1] // NCH
    own, other = [], []
    for c in range(NCH):
        near, far = gather_chunk(stale[:, c * width : (c + 1) * width])
        sums = partial_sums(a, near, far, degrees if c == 0 else None)
        mine, theirs = scatter_chunk(sums)
        own.append(mine)
        other.append(theirs)
    return finish(stale, w_self, w_neigh, own, other)


def solution(mesh):
    return jax.shard_map(
        on_device,
        mesh=mesh,
        in_specs=(
            P(("blk", "rep"), None),
            P(),
            P(),
            P("blk", "rep", None, None, None, None),
            P("blk", "rep", None, None),
            P("blk", "rep", None),
        ),
        out_specs=P(("blk", "rep"), None),
        check_vma=False,
    )
```

```python
import functools

import jax
import jax.numpy as jnp
from jax import lax
from jax.experimental import pallas as pl
from jax.experimental.pallas import tpu as pltpu
from jax.sharding import PartitionSpec as P

TILE = 128
OFFSETS = ((0, 0), (1, 0), (1, 1), (1, 3), (1, 2), (0, 2), (0, 1), (0, 3))


def blk_at(index, dx, dy, dc):
    x, y, c = index >> 3, (index >> 1) & 3, index & 1
    return (((x + dx) & 1) << 3) | (((y + dy) & 3) << 1) | ((c + dc) & 1)


def rep_at(index, dz, dx):
    return (((index >> 1) + dz) % 8) * 2 + ((index & 1) + dx) % 2


def from_blk(value, dx, dy, dc):
    return lax.ppermute(value, "blk", [(blk_at(i, dx, dy, dc), i) for i in range(16)])


def to_rep(value, dz, dx):
    return lax.ppermute(value, "rep", [(i, rep_at(i, dz, dx)) for i in range(16)])


def place_kernel(dc, meta, counts, places, tiles_ref, a_ref, sems):
    blk, my_z, my_x = meta[0], meta[1] >> 1, meta[1] & 1

    def copy(slot, source, k):
        place = places[source, k]
        row = ((((place >> 1) - my_z) & 7) << 1) | ((place + my_x) & 1)
        span = pl.ds(pl.multiple_of(row * TILE, TILE), TILE)
        return pltpu.make_async_copy(
            tiles_ref.at[source, k], a_ref.at[slot, span, :], sems.at[slot, k]
        )

    sources = [blk_at(blk, dx, dy, dc) for dx, dy in OFFSETS]
    for slot, source in enumerate(sources):
        a_ref[slot] = jnp.zeros(a_ref.shape[1:], a_ref.dtype)

        def start(k, carry):
            copy(slot, source, k).start()
            return carry

        lax.fori_loop(0, counts[source], start, 0)
    for slot, source in enumerate(sources):

        def wait(k, carry):
            copy(slot, source, k).wait()
            return carry

        lax.fori_loop(0, counts[source], wait, 0)


def place_tiles(dc, meta, counts, places, tiles):
    lists, cap = len(OFFSETS), tiles.shape[1]
    smem = pl.BlockSpec(memory_space=pltpu.SMEM)
    return pl.pallas_call(
        functools.partial(place_kernel, dc),
        in_specs=[smem, smem, smem, pl.BlockSpec(memory_space=pl.ANY)],
        out_specs=pl.BlockSpec(memory_space=pltpu.VMEM),
        out_shape=pltpu.VMEM((lists, 16 * TILE, TILE), jnp.bfloat16),
        scratch_shapes=[pltpu.SemaphoreType.DMA((lists, cap))],
        compiler_params=pltpu.CompilerParams(vmem_limit_bytes=1 << 20),
        cost_estimate=pl.CostEstimate(flops=1 << 20, transcendentals=0, bytes_accessed=7 << 20),
        name="place_tiles",
    )(meta, counts, places, pltpu.with_memory_space_constraint(tiles, pltpu.HBM))


def sum_kernel(slots, meta, a_near, a_far, near_ref, far_ref, *out_refs):
    my_z = meta[1] >> 1
    for slot, out_ref in zip(slots, out_refs):
        width = out_ref.shape[-1]
        span = slice(slot * 2 * TILE, (slot + 1) * 2 * TILE)
        result = jnp.zeros((2 * TILE, width), jnp.float32)
        degree = jnp.zeros((8, 2 * TILE), jnp.float32)
        for a_ref, source in ((a_near, near_ref), (a_far, far_ref)):
            left = jnp.concatenate([a_ref[j, span, :] for j in range(len(OFFSETS))], axis=1)
            result += jnp.dot(left, source[...], preferred_element_type=jnp.float32)
            degree += lax.dot_general(
                jnp.ones((8, left.shape[1]), left.dtype),
                left,
                (((1,), (1,)), ((), ())),
                preferred_element_type=jnp.float32,
            )
        result = result.astype(out_ref.dtype)
        mine = lax.broadcasted_iota(jnp.int32, (8, TILE), 0) == my_z
        for x in range(2):
            out_ref[x, :TILE, :] = result[x * TILE : (x + 1) * TILE]
            deg = jnp.where(mine, degree[:, x * TILE : (x + 1) * TILE], 0.0)
            pad = jnp.zeros((8, width - TILE), jnp.float32)
            out_ref[x, TILE:, :] = jnp.concatenate([deg, pad], axis=1).astype(out_ref.dtype)


def partial_sums(slots, meta, a_near, a_far, near, far):
    width = far.shape[1]
    shape = (2, TILE + 8, width)
    vmem = pl.BlockSpec(memory_space=pltpu.VMEM)
    return pl.pallas_call(
        functools.partial(sum_kernel, slots),
        in_specs=[pl.BlockSpec(memory_space=pltpu.SMEM)] + [vmem] * 4,
        out_specs=[vmem] * len(slots),
        out_shape=[jax.ShapeDtypeStruct(shape, jnp.bfloat16) for _ in slots],
        compiler_params=pltpu.CompilerParams(vmem_limit_bytes=8 << 20),
        cost_estimate=pl.CostEstimate(
            flops=len(slots) * 2 * 256 * 2048 * width,
            transcendentals=0,
            bytes_accessed=len(slots) << 20,
        ),
        name="partial_sums",
    )(meta, a_near, a_far, near, far)


def finish_kernel(stale_ref, w_self_ref, w_neigh_ref, zero_ref, *refs):
    out_ref = refs[-1]
    stale = stale_ref[...]
    total = zero_ref[0].astype(jnp.float32)
    for ref in refs[:-1]:
        total += ref[...].astype(jnp.float32)
    degree = jnp.sum(total[TILE:, :TILE], axis=0, keepdims=True)
    degree = jnp.broadcast_to(degree, (TILE, TILE)).T
    degree = jnp.concatenate([degree] * (stale.shape[1] // TILE), axis=1)
    mean = ((stale.astype(jnp.float32) + total[:TILE]) / (1.0 + degree)).astype(jnp.bfloat16)
    hidden = jnp.dot(stale, w_self_ref[...], preferred_element_type=jnp.float32) + jnp.dot(
        mean, w_neigh_ref[...], preferred_element_type=jnp.float32
    )
    active = jnp.maximum(hidden, 0.0)
    out = active * lax.rsqrt(jnp.mean(active * active, axis=-1, keepdims=True) + 1e-05)
    out_ref[...] = out.astype(out_ref.dtype)


def finish(stale, w_self, w_neigh, *parts):
    return pl.pallas_call(
        finish_kernel,
        out_shape=jax.ShapeDtypeStruct(stale.shape, jnp.bfloat16),
        compiler_params=pltpu.CompilerParams(vmem_limit_bytes=8 << 20),
        name="finish",
    )(stale, w_self, w_neigh, *parts)


def on_device(stale, w_self, w_neigh, tile_weights, tile_pos, tile_counts):
    meta = jnp.stack([lax.axis_index("blk"), lax.axis_index("rep")]).astype(jnp.int32)
    tables = (tile_counts[0, 0], tile_pos[0, 0], tile_weights[0, 0])

    blocks = [from_blk(stale, dx, dy, 0) for dx, dy in OFFSETS[1:]]
    a_near = place_tiles(0, meta, *tables)
    blocks, a_near = lax.optimization_barrier((blocks, a_near))
    near = jnp.concatenate([stale] + blocks, axis=0)
    far = from_blk(near, 0, 0, 1)
    gate, near = lax.optimization_barrier((meta, near))
    a_far = place_tiles(1, gate, *tables)
    args = (meta, a_near, a_far, near, far)

    (four,) = partial_sums((4,), *args)
    up = to_rep(four[0:1], 1, 0)
    down = to_rep(four[1:2], -1, 0)
    three, five = partial_sums((3, 5), *args)
    up = to_rep(jnp.concatenate([three[0:1] + up, three[1:2]], axis=0), 1, 0)
    down = to_rep(jnp.concatenate([five[0:1], five[1:2] + down], axis=0), -1, 0)
    two, six = partial_sums((2, 6), *args)
    up = to_rep(two + up, 1, 0)
    down = to_rep(six + down, -1, 0)
    one, seven = partial_sums((1, 7), *args)
    up = one + up
    down = seven + down
    up_other, down_other = to_rep(up[1], 1, 0), to_rep(down[1], -1, 0)
    up_own, down_own = to_rep(up[0], 1, 0), to_rep(down[0], -1, 0)
    (zero,) = partial_sums((0,), *args)
    wide = jnp.float32
    other = zero[1].astype(wide) + up_other.astype(wide) + down_other.astype(wide)
    other = to_rep(other.astype(jnp.bfloat16), 0, 1)
    return finish(stale, w_self, w_neigh, zero, up_own, down_own, other)


def solution(mesh):
    return jax.shard_map(
        on_device,
        mesh=mesh,
        in_specs=(
            P(("blk", "rep"), None),
            P(),
            P(),
            P("blk", "rep", None, None, None, None),
            P("blk", "rep", None, None),
            P("blk", "rep", None),
        ),
        out_specs=P(("blk", "rep"), None),
        check_vma=False,
    )
```

```python
import functools

import jax
import jax.numpy as jnp
from jax import lax
from jax.experimental import pallas as pl
from jax.experimental.pallas import tpu as pltpu
from jax.sharding import PartitionSpec as P

TILE = 128
OFFSETS = ((0, 0), (1, 2), (0, 2), (1, 1), (1, 3), (1, 0), (0, 1), (0, 3))


def blk_at(index, dx, dy, dc):
    x, y, c = index >> 3, (index >> 1) & 3, index & 1
    return (((x + dx) & 1) << 3) | (((y + dy) & 3) << 1) | ((c + dc) & 1)


def rep_at(index, dz, dx):
    return (((index >> 1) + dz) % 8) * 2 + ((index & 1) + dx) % 2


def from_blk(value, dx, dy, dc):
    return lax.ppermute(value, "blk", [(blk_at(i, dx, dy, dc), i) for i in range(16)])


def to_rep(value, dz, dx):
    return lax.ppermute(value, "rep", [(i, rep_at(i, dz, dx)) for i in range(16)])


def place_kernel(dc, meta, counts, places, tiles_ref, a_ref, sems):
    blk, first, flip = meta[0], meta[1] & 14, meta[1] & 1
    sources = [blk_at(blk, dx, dy, dc) for dx, dy in OFFSETS]
    for slot, source in enumerate(sources):
        a_ref[slot] = jnp.zeros(a_ref.shape[1:], a_ref.dtype)

        def start(k, carry):
            row = ((places[source, k] - first) & 15) ^ flip
            span = pl.ds(pl.multiple_of(row * TILE, TILE), TILE)
            pltpu.make_async_copy(
                tiles_ref.at[source, k], a_ref.at[slot, span, :], sems.at[slot, k]
            ).start()
            return carry

        lax.fori_loop(0, counts[source], start, 0)
    for slot, source in enumerate(sources):

        def wait(k, carry):
            pltpu.make_async_copy(
                tiles_ref.at[0, 0], a_ref.at[slot, :TILE, :], sems.at[slot, k]
            ).wait()
            return carry

        lax.fori_loop(0, counts[source], wait, 0)


def place_tiles(dc, meta, counts, places, tiles):
    lists, cap = len(OFFSETS), tiles.shape[1]
    smem = pl.BlockSpec(memory_space=pltpu.SMEM)
    return pl.pallas_call(
        functools.partial(place_kernel, dc),
        in_specs=[smem, smem, smem, pl.BlockSpec(memory_space=pl.ANY)],
        out_specs=pl.BlockSpec(memory_space=pltpu.VMEM),
        out_shape=pltpu.VMEM((lists, 16 * TILE, TILE), jnp.bfloat16),
        scratch_shapes=[pltpu.SemaphoreType.DMA((lists, cap))],
        compiler_params=pltpu.CompilerParams(vmem_limit_bytes=1 << 20),
        cost_estimate=pl.CostEstimate(flops=1 << 20, transcendentals=0, bytes_accessed=7 << 20),
        name="place_tiles",
    )(meta, counts, places, pltpu.with_memory_space_constraint(tiles, pltpu.HBM))


def sum_kernel(slots, meta, a_near, a_far, near_ref, far_ref, *out_refs):
    my_z = meta[1] >> 1
    width = near_ref.shape[-1]
    mine = lax.broadcasted_iota(jnp.int32, (8, TILE), 0) == my_z
    diagonal = lax.broadcasted_iota(jnp.int32, (TILE, TILE), 0) == lax.broadcasted_iota(
        jnp.int32, (TILE, TILE), 1
    )
    for index, slot in enumerate(slots):
        span = slice(slot * 2 * TILE, (slot + 1) * 2 * TILE)
        result = jnp.zeros((2 * TILE, width), jnp.float32)
        weight = jnp.zeros((2 * TILE, TILE), jnp.float32)
        for a_ref, source in ((a_near, near_ref), (a_far, far_ref)):
            pieces = [a_ref[j, span, :] for j in range(len(OFFSETS))]
            left = jnp.concatenate(pieces, axis=1)
            result += jnp.dot(left, source[...], preferred_element_type=jnp.float32)
            for piece in pieces:
                weight += piece.astype(jnp.float32)
        degree = jnp.sum(weight, axis=1, keepdims=True)
        for x in range(2):
            out_ref = out_refs[2 * index + x]
            rows = slice(x * TILE, (x + 1) * TILE)
            out_ref[:TILE, :] = result[rows].astype(out_ref.dtype)
            deg = jnp.sum(jnp.where(diagonal, degree[rows], 0.0), axis=0, keepdims=True)
            deg = jnp.where(mine, deg, 0.0)
            pad = jnp.zeros((8, width - TILE), jnp.float32)
            out_ref[TILE:, :] = jnp.concatenate([deg, pad], axis=1).astype(out_ref.dtype)


def partial_sums(slots, meta, a_near, a_far, near, far):
    width = far.shape[1]
    vmem = pl.BlockSpec(memory_space=pltpu.VMEM)
    outs = 2 * len(slots)
    return pl.pallas_call(
        functools.partial(sum_kernel, slots),
        in_specs=[pl.BlockSpec(memory_space=pltpu.SMEM)] + [vmem] * 4,
        out_specs=[vmem] * outs,
        out_shape=[jax.ShapeDtypeStruct((TILE + 8, width), jnp.bfloat16)] * outs,
        compiler_params=pltpu.CompilerParams(vmem_limit_bytes=8 << 20),
        cost_estimate=pl.CostEstimate(
            flops=len(slots) * 2 * 256 * 2048 * width,
            transcendentals=0,
            bytes_accessed=len(slots) << 20,
        ),
        name="partial_sums",
    )(meta, a_near, a_far, near, far)


def finish_kernel(stale_ref, w_self_ref, w_neigh_ref, zero_ref, *refs):
    out_ref = refs[-1]
    stale = stale_ref[...]
    total = zero_ref[...].astype(jnp.float32)
    for ref in refs[:-1]:
        total += ref[...].astype(jnp.float32)
    degree = jnp.sum(total[TILE:, :TILE], axis=0, keepdims=True)
    degree = jnp.broadcast_to(degree, (TILE, TILE)).T
    degree = jnp.concatenate([degree] * (stale.shape[1] // TILE), axis=1)
    mean = ((stale.astype(jnp.float32) + total[:TILE]) / (1.0 + degree)).astype(jnp.bfloat16)
    hidden = jnp.dot(stale, w_self_ref[...], preferred_element_type=jnp.float32) + jnp.dot(
        mean, w_neigh_ref[...], preferred_element_type=jnp.float32
    )
    active = jnp.maximum(hidden, 0.0)
    out = active * lax.rsqrt(jnp.mean(active * active, axis=-1, keepdims=True) + 1e-05)
    out_ref[...] = out.astype(out_ref.dtype)


def finish(stale, w_self, w_neigh, *parts):
    return pl.pallas_call(
        finish_kernel,
        out_shape=jax.ShapeDtypeStruct(stale.shape, jnp.bfloat16),
        compiler_params=pltpu.CompilerParams(vmem_limit_bytes=8 << 20),
        name="finish",
    )(stale, w_self, w_neigh, *parts)


def on_device(stale, w_self, w_neigh, tile_weights, tile_pos, tile_counts):
    meta = jnp.stack([lax.axis_index("blk"), lax.axis_index("rep")]).astype(jnp.int32)
    tables = (tile_counts[0, 0], tile_pos[0, 0], tile_weights[0, 0])

    blocks = [from_blk(stale, dx, dy, 0) for dx, dy in OFFSETS[1:]]
    a_near = place_tiles(0, meta, *tables)
    blocks, a_near = lax.optimization_barrier((blocks, a_near))
    near = jnp.concatenate([stale] + blocks, axis=0)
    far = from_blk(near, 0, 0, 1)
    gate, near = lax.optimization_barrier((meta, near))
    a_far = place_tiles(1, gate, *tables)
    args = (meta, a_near, a_far, near, far)

    own, other = partial_sums((4,), *args)
    up_other = to_rep(other, 1, 0)
    down_own = to_rep(own, -1, 0)
    three_own, three_other, five_own, five_other = partial_sums((3, 5), *args)
    down_other = to_rep(five_other, -1, 0)
    up_own = to_rep(three_own, 1, 0)
    up_other = to_rep(three_other + up_other, 1, 0)
    down_own = to_rep(five_own + down_own, -1, 0)
    for slots in ((2, 6), (1, 7)):
        low_own, low_other, high_own, high_other = partial_sums(slots, *args)
        down_other = to_rep(high_other + down_other, -1, 0)
        up_own = to_rep(low_own + up_own, 1, 0)
        up_other = to_rep(low_other + up_other, 1, 0)
        down_own = to_rep(high_own + down_own, -1, 0)
    own, other = partial_sums((0,), *args)
    other = sum(part.astype(jnp.float32) for part in (other, up_other, down_other))
    other = to_rep(other.astype(jnp.bfloat16), 0, 1)
    return finish(stale, w_self, w_neigh, own, up_own, down_own, other)


def solution(mesh):
    return jax.shard_map(
        on_device,
        mesh=mesh,
        in_specs=(
            P(("blk", "rep"), None),
            P(),
            P(),
            P("blk", "rep", None, None, None, None),
            P("blk", "rep", None, None),
            P("blk", "rep", None),
        ),
        out_specs=P(("blk", "rep"), None),
        check_vma=False,
    )
```

```python
import functools

import jax
import jax.numpy as jnp
from jax import lax
from jax.experimental import pallas as pl
from jax.experimental.pallas import tpu as pltpu
from jax.sharding import PartitionSpec as P


TILE = 128
PAIRS = (((1, 2), (0, 1), (1, 3)), ((0, 2), (1, 1), (0, 3)))
SINGLE = (1, 0)


def blk_at(index, dx, dy, dc):
    x, y, c = index >> 3, (index >> 1) & 3, index & 1
    return (((x + dx) & 1) << 3) | (((y + dy) & 3) << 1) | ((c + dc) & 1)


def rep_at(index, dz, dx):
    return (((index >> 1) + dz) % 8) * 2 + ((index & 1) + dx) % 2


def from_pair(value, index):
    pairs = [(blk_at(i, *PAIRS[i & 1][index], 0), i) for i in range(16)]
    return lax.ppermute(value, "blk", pairs)


def from_single(value):
    return lax.ppermute(value, "blk", [(blk_at(i, *SINGLE, 0), i) for i in range(16)])


def from_other_core(value):
    return lax.ppermute(value, "blk", [(i, i ^ 1) for i in range(16)])


def to_rep(value, dz, dx):
    pairs = [
        (b * 16 + i, b * 16 + rep_at(i, -dz if b & 1 else dz, dx))
        for b in range(16)
        for i in range(16)
    ]
    return lax.ppermute(value, ("blk", "rep"), pairs)


def slot_sources(blk):
    def fetched(dc):
        found = []
        for index in range(3):
            for other in range(2):
                options = [blk_at(blk, *offsets[index], dc + other) for offsets in PAIRS]
                found.append(jnp.where(((blk + dc) & 1) == 0, *options))
        return found

    one = [blk_at(blk, *SINGLE, dc) for dc in range(2)]
    own = [blk_at(blk, 0, 0, dc) for dc in range(2)]
    return own + fetched(0) + one[:1] + fetched(1) + one[1:]


def place_kernel(meta, counts_hbm, places_hbm, tiles_ref, a_ref, counts, places, table_sems, sems):
    tables = [
        pltpu.make_async_copy(counts_hbm, counts, table_sems.at[0]),
        pltpu.make_async_copy(places_hbm, places, table_sems.at[1]),
    ]
    for table in tables:
        table.start()
    blk, my_z, my_x = meta[0], meta[1] >> 1, meta[1] & 1
    sign = 1 - 2 * (blk & 1)
    sources = slot_sources(blk)
    for slot, source in enumerate(sources):
        a_ref[slot] = jnp.zeros(a_ref.shape[1:], a_ref.dtype)
        if slot == 0:
            for table in tables:
                table.wait()

        def start(k, carry):
            place = places[k, 0, source]
            row = (((((place >> 1) - my_z) * sign) & 7) << 1) | ((place ^ my_x) & 1)
            span = pl.ds(pl.multiple_of(row * TILE, TILE), TILE)
            pltpu.make_async_copy(
                tiles_ref.at[source, k], a_ref.at[slot, span, :], sems.at[slot, k]
            ).start()
            return carry

        lax.fori_loop(0, counts[source], start, 0)
    for slot, source in enumerate(sources):

        def wait(k, carry):
            pltpu.make_async_copy(
                tiles_ref.at[0, 0], a_ref.at[slot, :TILE, :], sems.at[slot, k]
            ).wait()
            return carry

        lax.fori_loop(0, counts[source], wait, 0)


def place_tiles(meta, counts, places, tiles):
    lists, cap = tiles.shape[:2]
    whole = pl.BlockSpec(memory_space=pl.ANY)
    hbm = [pltpu.with_memory_space_constraint(x, pltpu.HBM) for x in (counts, places, tiles)]
    return pl.pallas_call(
        place_kernel,
        in_specs=[pl.BlockSpec(memory_space=pltpu.SMEM), whole, whole, whole],
        out_specs=pl.BlockSpec(memory_space=pltpu.VMEM),
        out_shape=pltpu.VMEM((lists, 16 * TILE, TILE), jnp.bfloat16),
        scratch_shapes=[
            pltpu.SMEM(counts.shape, jnp.int32),
            pltpu.SMEM(places.shape, jnp.int32),
            pltpu.SemaphoreType.DMA((2,)),
            pltpu.SemaphoreType.DMA((lists, cap)),
        ],
        compiler_params=pltpu.CompilerParams(vmem_limit_bytes=1 << 20),
        cost_estimate=pl.CostEstimate(flops=1 << 20, transcendentals=0, bytes_accessed=14 << 20),
        name="place_tiles",
    )(meta, *hbm)


def near_kernel(first, a_ref, *refs):
    out_ref = refs[-1]
    sources, partials = refs[:2], refs[2:-1]
    right = jnp.concatenate([ref[...] for ref in sources], axis=0)
    for slot in range(out_ref.shape[0]):
        span = slice(slot * 2 * TILE, (slot + 1) * 2 * TILE)
        left = jnp.concatenate([a_ref[first + j, span, :] for j in range(4)], axis=1)
        result = jnp.dot(left, right, preferred_element_type=jnp.float32)
        for partial in partials:
            result += partial[slot]
        out_ref[slot] = result


def near_sums(first, a, sources, *partials):
    vmem = pl.BlockSpec(memory_space=pltpu.VMEM)
    width = sources[0].shape[1]
    return pl.pallas_call(
        functools.partial(near_kernel, first),
        in_specs=[vmem] * (3 + len(partials)),
        out_specs=vmem,
        out_shape=pltpu.VMEM((8, 2 * TILE, width), jnp.float32),
        compiler_params=pltpu.CompilerParams(vmem_limit_bytes=4 << 20),
        cost_estimate=pl.CostEstimate(
            flops=2 * 2048 * 512 * width, transcendentals=0, bytes_accessed=6 << 20
        ),
        name="near_sums",
    )(a, *sources, *partials)


def far_kernel(slots, planes, meta, a_ref, partial_ref, *refs):
    my_z = meta[1] >> 1
    sources, out_refs = refs[:4], refs[4:]
    width = sources[0].shape[-1]
    right = jnp.concatenate([ref[...] for ref in sources], axis=0)
    mine = lax.broadcasted_iota(jnp.int32, (8, TILE), 0) == my_z
    diagonal = lax.broadcasted_iota(jnp.int32, (TILE, TILE), 0) == lax.broadcasted_iota(
        jnp.int32, (TILE, TILE), 1
    )
    out_refs = list(out_refs)
    for slot in slots:
        first, rows = planes[0] * TILE, len(planes) * TILE
        span = slice(slot * 2 * TILE + first, slot * 2 * TILE + first + rows)
        pieces = [a_ref[j, span, :] for j in range(a_ref.shape[0])]
        weight = jnp.zeros((rows, TILE), jnp.float32)
        for piece in pieces:
            weight += piece.astype(jnp.float32)
        left = jnp.concatenate(pieces[8:], axis=1)
        result = partial_ref[slot, first : first + rows] + jnp.dot(
            left, right, preferred_element_type=jnp.float32
        )
        degree = jnp.sum(weight, axis=1, keepdims=True)
        for x in range(len(planes)):
            out_ref = out_refs.pop(0)
            part = slice(x * TILE, (x + 1) * TILE)
            out_ref[:TILE, :] = result[part].astype(out_ref.dtype)
            deg = jnp.sum(jnp.where(diagonal, degree[part], 0.0), axis=0, keepdims=True)
            deg = jnp.where(mine, deg, 0.0)
            pad = jnp.zeros((8, width - TILE), jnp.float32)
            out_ref[TILE:, :] = jnp.concatenate([deg, pad], axis=1).astype(out_ref.dtype)


def far_sums(slots, planes, meta, a, partial, *sources):
    width = sources[0].shape[1]
    vmem = pl.BlockSpec(memory_space=pltpu.VMEM)
    outs = len(planes) * len(slots)
    return pl.pallas_call(
        functools.partial(far_kernel, slots, planes),
        in_specs=[pl.BlockSpec(memory_space=pltpu.SMEM)] + [vmem] * 6,
        out_specs=[vmem] * outs,
        out_shape=[jax.ShapeDtypeStruct((TILE + 8, width), jnp.bfloat16)] * outs,
        compiler_params=pltpu.CompilerParams(vmem_limit_bytes=8 << 20),
        cost_estimate=pl.CostEstimate(
            flops=outs * 2 * TILE * 1024 * width, transcendentals=0, bytes_accessed=outs << 19
        ),
        name="far_sums",
    )(meta, a, partial, *sources)


def prepare_kernel(stale_ref, w_self_ref, *refs):
    hidden_ref, total_ref = refs[-2:]
    stale = stale_ref[...]
    hidden_ref[...] = jnp.dot(stale, w_self_ref[...], preferred_element_type=jnp.float32)
    total = sum(ref[...].astype(jnp.float32) for ref in refs[:-2])
    total_ref[:TILE, :] = total[:TILE] + stale.astype(jnp.float32)
    total_ref[TILE:, :] = total[TILE:]


def prepare(stale, w_self, *parts):
    rows, width = parts[0].shape
    return pl.pallas_call(
        prepare_kernel,
        out_shape=[
            jax.ShapeDtypeStruct(stale.shape, jnp.float32),
            jax.ShapeDtypeStruct((rows, width), jnp.float32),
        ],
        compiler_params=pltpu.CompilerParams(vmem_limit_bytes=4 << 20),
        name="prepare",
    )(stale, w_self, *parts)


def finish_kernel(hidden_ref, total_ref, other_ref, w_neigh_ref, out_ref):
    total = total_ref[...] + other_ref[...].astype(jnp.float32)
    degree = jnp.sum(total[TILE:, :TILE], axis=0, keepdims=True)
    degree = jnp.broadcast_to(degree, (TILE, TILE)).T
    degree = jnp.concatenate([degree] * (total.shape[1] // TILE), axis=1)
    mean = (total[:TILE] / (1.0 + degree)).astype(jnp.bfloat16)
    hidden = hidden_ref[...] + jnp.dot(
        mean, w_neigh_ref[...], preferred_element_type=jnp.float32
    )
    active = jnp.maximum(hidden, 0.0)
    out = active * lax.rsqrt(jnp.mean(active * active, axis=-1, keepdims=True) + 1e-05)
    out_ref[...] = out.astype(out_ref.dtype)


def finish(hidden, total, other, w_neigh):
    return pl.pallas_call(
        finish_kernel,
        out_shape=jax.ShapeDtypeStruct(hidden.shape, jnp.bfloat16),
        compiler_params=pltpu.CompilerParams(vmem_limit_bytes=4 << 20),
        name="finish",
    )(hidden, total, other, w_neigh)


def refresh(stale, w_self, w_neigh, tile_weights, tile_pos, tile_counts):
    meta = jnp.stack([lax.axis_index("blk"), lax.axis_index("rep")]).astype(jnp.int32)
    places = jnp.transpose(tile_pos, (0, 3, 1, 2))[0]
    mate = from_other_core(stale)
    single = from_single(stale)
    own_pair = jnp.concatenate([stale, mate], axis=0)
    received = []
    for index in range(3):
        received.append(from_pair(own_pair, index))
    a = place_tiles(meta, tile_counts[0, 0], places, tile_weights[0, 0])
    first, second, third = received
    first, a = lax.optimization_barrier((first, a))
    first_far = from_other_core(first)
    partial = near_sums(0, a, (own_pair, first))
    second, third, single, partial = lax.optimization_barrier((second, third, single, partial))
    second_far = from_other_core(second)
    late_far = from_other_core(jnp.concatenate([third, single], axis=0))
    partial = near_sums(4, a, (second, third), partial)
    args = (meta, a, partial, single, first_far, second_far, late_far)
    both = (0, 1)

    def hop(value, dz, dx=0):
        return to_rep(value, dz, dx)

    own, other = far_sums((4,), both, *args)
    up_other = hop(other, 1)
    down_own = hop(own, -1)
    three_own, three_other, five_own, five_other = far_sums((3, 5), both, *args)
    down_other = hop(five_other, -1)
    up_own = hop(three_own, 1)
    up_other = hop(three_other + up_other, 1)
    down_own = hop(five_own + down_own, -1)
    for slots in ((2, 6), (1, 7)):
        low_own, low_other, high_own, high_other = far_sums(slots, both, *args)
        down_other = hop(high_other + down_other, -1)
        up_own = hop(low_own + up_own, 1)
        up_other = hop(low_other + up_other, 1)
        down_own = hop(high_own + down_own, -1)
    (other,) = far_sums((0,), (1,), *args)
    other = sum(part.astype(jnp.float32) for part in (other, up_other, down_other))
    other = hop(other.astype(jnp.bfloat16), 0, 1)
    (own,) = far_sums((0,), (0,), *args)
    hidden, total = prepare(stale, w_self, own, up_own, down_own)
    return finish(hidden, total, other, w_neigh)


def solution(mesh):
    return jax.shard_map(
        refresh,
        mesh=mesh,
        in_specs=(
            P(("blk", "rep"), None),
            P(),
            P(),
            P("blk", "rep", None, None, None, None),
            P("blk", "rep", None, None),
            P("blk", "rep", None),
        ),
        out_specs=P(("blk", "rep"), None),
        check_vma=False,
    )
```

```python
import functools

import jax
import jax.numpy as jnp
from jax import lax
from jax.experimental import pallas as pl
from jax.experimental.pallas import tpu as pltpu
from jax.sharding import PartitionSpec as P


TILE = 128
PAIRS = (((1, 0), (0, 2), (1, 1)), ((0, 1), (1, 3), (0, 3)))
SINGLE = (1, 2)


def blk_at(index, dx, dy, dc):
    x, y, c = index >> 3, (index >> 1) & 3, index & 1
    return (((x + dx) & 1) << 3) | (((y + dy) & 3) << 1) | ((c + dc) & 1)


def rep_at(index, dz, dx):
    return (((index >> 1) + dz) % 8) * 2 + ((index & 1) + dx) % 2


def from_pair(value, index):
    pairs = [(blk_at(i, *PAIRS[i & 1][index], 0), i) for i in range(16)]
    return lax.ppermute(value, "blk", pairs)


def from_single(value):
    return lax.ppermute(value, "blk", [(blk_at(i, *SINGLE, 0), i) for i in range(16)])


def from_other_core(value):
    return lax.ppermute(value, "blk", [(i, i ^ 1) for i in range(16)])


def to_rep(value, dz, dx):
    pairs = [
        (b * 16 + i, b * 16 + rep_at(i, -dz if b & 1 else dz, dx))
        for b in range(16)
        for i in range(16)
    ]
    return lax.ppermute(value, ("blk", "rep"), pairs)


def slot_sources(blk):
    def fetched(dc):
        found = []
        for index in range(3):
            for other in range(2):
                options = [blk_at(blk, *offsets[index], dc + other) for offsets in PAIRS]
                found.append(jnp.where(((blk + dc) & 1) == 0, *options))
        return found

    one = [blk_at(blk, *SINGLE, dc) for dc in range(2)]
    own = [blk_at(blk, 0, 0, dc) for dc in range(2)]
    return own + fetched(0) + one[:1] + fetched(1) + one[1:]


def place_kernel(meta, counts_hbm, places_hbm, tiles_ref, a_ref, counts, places, table_sems, sems):
    tables = [
        pltpu.make_async_copy(counts_hbm, counts, table_sems.at[0]),
        pltpu.make_async_copy(places_hbm, places, table_sems.at[1]),
    ]
    for table in tables:
        table.start()
    blk, my_z, my_x = meta[0], meta[1] >> 1, meta[1] & 1
    sign = 1 - 2 * (blk & 1)
    sources = slot_sources(blk)
    for slot, source in enumerate(sources):
        a_ref[slot] = jnp.zeros(a_ref.shape[1:], a_ref.dtype)
        if slot == 0:
            for table in tables:
                table.wait()

        def start(k, carry):
            place = places[k, 0, source]
            row = (((((place >> 1) - my_z) * sign) & 7) << 1) | ((place ^ my_x) & 1)
            span = pl.ds(pl.multiple_of(row * TILE, TILE), TILE)
            pltpu.make_async_copy(
                tiles_ref.at[source, k], a_ref.at[slot, span, :], sems.at[slot, k]
            ).start()
            return carry

        lax.fori_loop(0, counts[source], start, 0)
    for slot, source in enumerate(sources):

        def wait(k, carry):
            pltpu.make_async_copy(
                tiles_ref.at[0, 0], a_ref.at[slot, :TILE, :], sems.at[slot, k]
            ).wait()
            return carry

        lax.fori_loop(0, counts[source], wait, 0)


def place_tiles(meta, counts, places, tiles):
    lists, cap = tiles.shape[:2]
    whole = pl.BlockSpec(memory_space=pl.ANY)
    hbm = [pltpu.with_memory_space_constraint(x, pltpu.HBM) for x in (counts, places, tiles)]
    return pl.pallas_call(
        place_kernel,
        in_specs=[pl.BlockSpec(memory_space=pltpu.SMEM), whole, whole, whole],
        out_specs=pl.BlockSpec(memory_space=pltpu.VMEM),
        out_shape=pltpu.VMEM((lists, 16 * TILE, TILE), jnp.bfloat16),
        scratch_shapes=[
            pltpu.SMEM(counts.shape, jnp.int32),
            pltpu.SMEM(places.shape, jnp.int32),
            pltpu.SemaphoreType.DMA((2,)),
            pltpu.SemaphoreType.DMA((lists, cap)),
        ],
        compiler_params=pltpu.CompilerParams(vmem_limit_bytes=1 << 20),
        cost_estimate=pl.CostEstimate(flops=1 << 20, transcendentals=0, bytes_accessed=14 << 20),
        name="place_tiles",
    )(meta, *hbm)


def near_kernel(first, a_ref, *refs):
    out_ref = refs[-1]
    sources, partials = refs[:2], refs[2:-1]
    right = jnp.concatenate([ref[...] for ref in sources], axis=0)
    for slot in range(out_ref.shape[0]):
        span = slice(slot * 2 * TILE, (slot + 1) * 2 * TILE)
        left = jnp.concatenate([a_ref[first + j, span, :] for j in range(4)], axis=1)
        result = jnp.dot(left, right, preferred_element_type=jnp.float32)
        for partial in partials:
            result += partial[slot]
        out_ref[slot] = result


def near_sums(first, a, sources, *partials):
    vmem = pl.BlockSpec(memory_space=pltpu.VMEM)
    width = sources[0].shape[1]
    return pl.pallas_call(
        functools.partial(near_kernel, first),
        in_specs=[vmem] * (3 + len(partials)),
        out_specs=vmem,
        out_shape=pltpu.VMEM((8, 2 * TILE, width), jnp.float32),
        compiler_params=pltpu.CompilerParams(vmem_limit_bytes=4 << 20),
        cost_estimate=pl.CostEstimate(
            flops=2 * 2048 * 512 * width, transcendentals=0, bytes_accessed=6 << 20
        ),
        name="near_sums",
    )(a, *sources, *partials)


def far_kernel(slots, planes, meta, a_ref, partial_ref, *refs):
    my_z = meta[1] >> 1
    sources, out_refs = refs[:4], refs[4:]
    width = sources[0].shape[-1]
    right = jnp.concatenate([ref[...] for ref in sources], axis=0)
    mine = lax.broadcasted_iota(jnp.int32, (8, TILE), 0) == my_z
    diagonal = lax.broadcasted_iota(jnp.int32, (TILE, TILE), 0) == lax.broadcasted_iota(
        jnp.int32, (TILE, TILE), 1
    )
    out_refs = list(out_refs)
    for slot in slots:
        first, rows = planes[0] * TILE, len(planes) * TILE
        span = slice(slot * 2 * TILE + first, slot * 2 * TILE + first + rows)
        pieces = [a_ref[j, span, :] for j in range(a_ref.shape[0])]
        weight = jnp.zeros((rows, TILE), jnp.float32)
        for piece in pieces:
            weight += piece.astype(jnp.float32)
        left = jnp.concatenate(pieces[8:], axis=1)
        result = partial_ref[slot, first : first + rows] + jnp.dot(
            left, right, preferred_element_type=jnp.float32
        )
        degree = jnp.sum(weight, axis=1, keepdims=True)
        for x in range(len(planes)):
            out_ref = out_refs.pop(0)
            part = slice(x * TILE, (x + 1) * TILE)
            out_ref[:TILE, :] = result[part].astype(out_ref.dtype)
            deg = jnp.sum(jnp.where(diagonal, degree[part], 0.0), axis=0, keepdims=True)
            deg = jnp.where(mine, deg, 0.0)
            pad = jnp.zeros((8, width - TILE), jnp.float32)
            out_ref[TILE:, :] = jnp.concatenate([deg, pad], axis=1).astype(out_ref.dtype)


def far_sums(slots, planes, meta, a, partial, *sources):
    width = sources[0].shape[1]
    vmem = pl.BlockSpec(memory_space=pltpu.VMEM)
    outs = len(planes) * len(slots)
    return pl.pallas_call(
        functools.partial(far_kernel, slots, planes),
        in_specs=[pl.BlockSpec(memory_space=pltpu.SMEM)] + [vmem] * 6,
        out_specs=[vmem] * outs,
        out_shape=[jax.ShapeDtypeStruct((TILE + 8, width), jnp.bfloat16)] * outs,
        compiler_params=pltpu.CompilerParams(vmem_limit_bytes=8 << 20),
        cost_estimate=pl.CostEstimate(
            flops=outs * 2 * TILE * 1024 * width, transcendentals=0, bytes_accessed=outs << 19
        ),
        name="far_sums",
    )(meta, a, partial, *sources)


def prepare_kernel(stale_ref, w_self_ref, *refs):
    hidden_ref, total_ref = refs[-2:]
    stale = stale_ref[...]
    hidden_ref[...] = jnp.dot(stale, w_self_ref[...], preferred_element_type=jnp.float32)
    total = sum(ref[...].astype(jnp.float32) for ref in refs[:-2])
    total_ref[:TILE, :] = total[:TILE] + stale.astype(jnp.float32)
    total_ref[TILE:, :] = total[TILE:]


def prepare(stale, w_self, *parts):
    rows, width = parts[0].shape
    return pl.pallas_call(
        prepare_kernel,
        out_shape=[
            jax.ShapeDtypeStruct(stale.shape, jnp.float32),
            jax.ShapeDtypeStruct((rows, width), jnp.float32),
        ],
        compiler_params=pltpu.CompilerParams(vmem_limit_bytes=4 << 20),
        name="prepare",
    )(stale, w_self, *parts)


def finish_kernel(hidden_ref, total_ref, other_ref, w_neigh_ref, out_ref):
    total = total_ref[...] + other_ref[...].astype(jnp.float32)
    scale = 1.0 / (1.0 + jnp.sum(total[TILE:, :TILE], axis=0, keepdims=True))
    scale = jnp.broadcast_to(scale, (TILE, TILE)).T
    scale = jnp.concatenate([scale] * (total.shape[1] // TILE), axis=1)
    mean = (total[:TILE] * scale).astype(jnp.bfloat16)
    hidden = hidden_ref[...] + jnp.dot(
        mean, w_neigh_ref[...], preferred_element_type=jnp.float32
    )
    active = jnp.maximum(hidden, 0.0)
    out = active * lax.rsqrt(jnp.mean(active * active, axis=-1, keepdims=True) + 1e-05)
    out_ref[...] = out.astype(out_ref.dtype)


def finish(hidden, total, other, w_neigh):
    return pl.pallas_call(
        finish_kernel,
        out_shape=jax.ShapeDtypeStruct(hidden.shape, jnp.bfloat16),
        compiler_params=pltpu.CompilerParams(vmem_limit_bytes=4 << 20),
        name="finish",
    )(hidden, total, other, w_neigh)


def refresh(stale, w_self, w_neigh, tile_weights, tile_pos, tile_counts):
    meta = jnp.stack([lax.axis_index("blk"), lax.axis_index("rep")]).astype(jnp.int32)
    places = jnp.transpose(tile_pos, (0, 3, 1, 2))[0]
    mate = from_other_core(stale)
    single = from_single(stale)
    own_pair = jnp.concatenate([stale, mate], axis=0)
    received = []
    for index in range(3):
        received.append(from_pair(own_pair, index))
    a = place_tiles(meta, tile_counts[0, 0], places, tile_weights[0, 0])
    first, second, third = received
    first, a = lax.optimization_barrier((first, a))
    first_far = from_other_core(first)
    partial = near_sums(0, a, (own_pair, first))
    second, third, single, partial = lax.optimization_barrier((second, third, single, partial))
    second_far = from_other_core(second)
    late_far = from_other_core(jnp.concatenate([third, single], axis=0))
    partial = near_sums(4, a, (second, third), partial)
    args = (meta, a, partial, single, first_far, second_far, late_far)
    both = (0, 1)

    def hop(value, dz, dx=0):
        return to_rep(value, dz, dx)

    own, other = far_sums((4,), both, *args)
    up_other = hop(other, 1)
    down_own = hop(own, -1)
    three_own, three_other, five_own, five_other = far_sums((3, 5), both, *args)
    down_other = hop(five_other, -1)
    up_own = hop(three_own, 1)
    up_other = hop(three_other + up_other, 1)
    down_own = hop(five_own + down_own, -1)
    for slots in ((2, 6), (1, 7)):
        low_own, low_other, high_own, high_other = far_sums(slots, both, *args)
        down_other = hop(high_other + down_other, -1)
        up_own = hop(low_own + up_own, 1)
        up_other = hop(low_other + up_other, 1)
        down_own = hop(high_own + down_own, -1)
    (other,) = far_sums((0,), (1,), *args)
    other = sum(part.astype(jnp.float32) for part in (other, up_other, down_other))
    other = hop(other.astype(jnp.bfloat16), 0, 1)
    (own,) = far_sums((0,), (0,), *args)
    hidden, total = prepare(stale, w_self, own, up_own, down_own)
    return finish(hidden, total, other, w_neigh)


def solution(mesh):
    return jax.shard_map(
        refresh,
        mesh=mesh,
        in_specs=(
            P(("blk", "rep"), None),
            P(),
            P(),
            P("blk", "rep", None, None, None, None),
            P("blk", "rep", None, None),
            P("blk", "rep", None),
        ),
        out_specs=P(("blk", "rep"), None),
        check_vma=False,
    )
```

```python
import functools

import jax
import jax.numpy as jnp
from jax import lax
from jax.experimental import pallas as pl
from jax.experimental.pallas import tpu as pltpu
from jax.sharding import PartitionSpec as P


TILE = 128
PAIRS = (((1, 0), (0, 2), (1, 1)), ((0, 1), (1, 3), (0, 3)))
SINGLE = (1, 2)


def blk_at(index, dx, dy, dc):
    x, y, c = index >> 3, (index >> 1) & 3, index & 1
    return (((x + dx) & 1) << 3) | (((y + dy) & 3) << 1) | ((c + dc) & 1)


def rep_at(index, dz, dx):
    return (((index >> 1) + dz) % 8) * 2 + ((index & 1) + dx) % 2


def from_pair(value, index):
    pairs = [(blk_at(i, *PAIRS[i & 1][index], 0), i) for i in range(16)]
    return lax.ppermute(value, "blk", pairs)


def from_single(value):
    return lax.ppermute(value, "blk", [(blk_at(i, *SINGLE, 0), i) for i in range(16)])


def from_other_core(value):
    return lax.ppermute(value, "blk", [(i, i ^ 1) for i in range(16)])


def to_rep(value, dz, dx):
    pairs = [
        (b * 16 + i, b * 16 + rep_at(i, -dz if b & 1 else dz, dx))
        for b in range(16)
        for i in range(16)
    ]
    return lax.ppermute(value, ("blk", "rep"), pairs)


def slot_sources(blk):
    def fetched(dc):
        found = []
        for index in range(3):
            for other in range(2):
                options = [blk_at(blk, *offsets[index], dc + other) for offsets in PAIRS]
                found.append(jnp.where(((blk + dc) & 1) == 0, *options))
        return found

    one = [blk_at(blk, *SINGLE, dc) for dc in range(2)]
    own = [blk_at(blk, 0, 0, dc) for dc in range(2)]
    return own + fetched(0) + one[:1] + fetched(1) + one[1:]


def place_kernel(meta, counts_hbm, places_hbm, tiles_ref, a_ref, counts, places, table_sems, sems):
    tables = [
        pltpu.make_async_copy(counts_hbm, counts, table_sems.at[0]),
        pltpu.make_async_copy(places_hbm, places, table_sems.at[1]),
    ]
    for table in tables:
        table.start()
    blk, my_z, my_x = meta[0], meta[1] >> 1, meta[1] & 1
    sign = 1 - 2 * (blk & 1)
    sources = slot_sources(blk)
    for slot, source in enumerate(sources):
        a_ref[slot] = jnp.zeros(a_ref.shape[1:], a_ref.dtype)
        if slot == 0:
            for table in tables:
                table.wait()

        def start(k, carry):
            place = places[k, 0, source]
            row = (((((place >> 1) - my_z) * sign) & 7) << 1) | ((place ^ my_x) & 1)
            span = pl.ds(pl.multiple_of(row * TILE, TILE), TILE)
            pltpu.make_async_copy(
                tiles_ref.at[source, k], a_ref.at[slot, span, :], sems.at[slot, k]
            ).start()
            return carry

        lax.fori_loop(0, counts[source], start, 0)
    for slot, source in enumerate(sources):

        def wait(k, carry):
            pltpu.make_async_copy(
                tiles_ref.at[0, 0], a_ref.at[slot, :TILE, :], sems.at[slot, k]
            ).wait()
            return carry

        lax.fori_loop(0, counts[source], wait, 0)


def place_tiles(meta, counts, places, tiles):
    lists, cap = tiles.shape[:2]
    whole = pl.BlockSpec(memory_space=pl.ANY)
    hbm = [pltpu.with_memory_space_constraint(x, pltpu.HBM) for x in (counts, places, tiles)]
    return pl.pallas_call(
        place_kernel,
        in_specs=[pl.BlockSpec(memory_space=pltpu.SMEM), whole, whole, whole],
        out_specs=pl.BlockSpec(memory_space=pltpu.VMEM),
        out_shape=pltpu.VMEM((lists, 16 * TILE, TILE), jnp.bfloat16),
        scratch_shapes=[
            pltpu.SMEM(counts.shape, jnp.int32),
            pltpu.SMEM(places.shape, jnp.int32),
            pltpu.SemaphoreType.DMA((2,)),
            pltpu.SemaphoreType.DMA((lists, cap)),
        ],
        compiler_params=pltpu.CompilerParams(vmem_limit_bytes=1 << 20),
        cost_estimate=pl.CostEstimate(flops=1 << 20, transcendentals=0, bytes_accessed=14 << 20),
        name="place_tiles",
    )(meta, *hbm)


def near_kernel(first, a_ref, *refs):
    out_ref = refs[-1]
    sources, partials = refs[:2], refs[2:-1]
    right = jnp.concatenate([ref[...] for ref in sources], axis=0)
    for slot in range(out_ref.shape[0]):
        span = slice(slot * 2 * TILE, (slot + 1) * 2 * TILE)
        left = jnp.concatenate([a_ref[first + j, span, :] for j in range(4)], axis=1)
        result = jnp.dot(left, right, preferred_element_type=jnp.float32)
        for partial in partials:
            result += partial[slot]
        out_ref[slot] = result


def near_sums(first, a, sources, *partials):
    vmem = pl.BlockSpec(memory_space=pltpu.VMEM)
    width = sources[0].shape[1]
    return pl.pallas_call(
        functools.partial(near_kernel, first),
        in_specs=[vmem] * (3 + len(partials)),
        out_specs=vmem,
        out_shape=pltpu.VMEM((8, 2 * TILE, width), jnp.float32),
        compiler_params=pltpu.CompilerParams(vmem_limit_bytes=4 << 20),
        cost_estimate=pl.CostEstimate(
            flops=2 * 2048 * 512 * width, transcendentals=0, bytes_accessed=6 << 20
        ),
        name="near_sums",
    )(a, *sources, *partials)


def far_kernel(slots, planes, meta, a_ref, partial_ref, *refs):
    my_z = meta[1] >> 1
    sources, out_refs = refs[:4], refs[4:]
    width = sources[0].shape[-1]
    right = jnp.concatenate([ref[...] for ref in sources], axis=0)
    mine = lax.broadcasted_iota(jnp.int32, (8, TILE), 0) == my_z
    diagonal = lax.broadcasted_iota(jnp.int32, (TILE, TILE), 0) == lax.broadcasted_iota(
        jnp.int32, (TILE, TILE), 1
    )
    out_refs = list(out_refs)
    for slot in slots:
        first, rows = planes[0] * TILE, len(planes) * TILE
        span = slice(slot * 2 * TILE + first, slot * 2 * TILE + first + rows)
        pieces = [a_ref[j, span, :] for j in range(a_ref.shape[0])]
        weight = jnp.zeros((rows, TILE), jnp.float32)
        for piece in pieces:
            weight += piece.astype(jnp.float32)
        left = jnp.concatenate(pieces[8:], axis=1)
        result = partial_ref[slot, first : first + rows] + jnp.dot(
            left, right, preferred_element_type=jnp.float32
        )
        degree = jnp.sum(weight, axis=1, keepdims=True)
        for x in range(len(planes)):
            out_ref = out_refs.pop(0)
            part = slice(x * TILE, (x + 1) * TILE)
            for c in range(width // TILE):
                columns = result[part, c * TILE : (c + 1) * TILE]
                out_ref[c * TILE : (c + 1) * TILE, :] = columns.astype(out_ref.dtype)
            deg = jnp.sum(jnp.where(diagonal, degree[part], 0.0), axis=0, keepdims=True)
            out_ref[width:, :] = jnp.where(mine, deg, 0.0).astype(out_ref.dtype)


def far_sums(slots, planes, meta, a, partial, *sources):
    width = sources[0].shape[1]
    vmem = pl.BlockSpec(memory_space=pltpu.VMEM)
    outs = len(planes) * len(slots)
    return pl.pallas_call(
        functools.partial(far_kernel, slots, planes),
        in_specs=[pl.BlockSpec(memory_space=pltpu.SMEM)] + [vmem] * 6,
        out_specs=[vmem] * outs,
        out_shape=[jax.ShapeDtypeStruct((width + 8, TILE), jnp.bfloat16)] * outs,
        compiler_params=pltpu.CompilerParams(vmem_limit_bytes=8 << 20),
        cost_estimate=pl.CostEstimate(
            flops=outs * 2 * TILE * 1024 * width, transcendentals=0, bytes_accessed=outs << 19
        ),
        name="far_sums",
    )(meta, a, partial, *sources)


def prepare_kernel(stale_ref, w_self_ref, *refs):
    hidden_ref, total_ref = refs[-2:]
    stale = stale_ref[...]
    hidden_ref[...] = jnp.dot(stale, w_self_ref[...], preferred_element_type=jnp.float32)
    total = sum(ref[...].astype(jnp.float32) for ref in refs[:-2])
    width = stale.shape[1]
    for c in range(width // TILE):
        span = slice(c * TILE, (c + 1) * TILE)
        total_ref[span, :] = total[span] + stale[:, span].astype(jnp.float32)
    total_ref[width:, :] = total[width:]


def prepare(stale, w_self, *parts):
    rows, width = parts[0].shape
    return pl.pallas_call(
        prepare_kernel,
        out_shape=[
            jax.ShapeDtypeStruct(stale.shape, jnp.float32),
            jax.ShapeDtypeStruct((rows, width), jnp.float32),
        ],
        compiler_params=pltpu.CompilerParams(vmem_limit_bytes=4 << 20),
        name="prepare",
    )(stale, w_self, *parts)


def finish_kernel(hidden_ref, total_ref, other_ref, w_neigh_ref, out_ref):
    total = total_ref[...] + other_ref[...].astype(jnp.float32)
    width = hidden_ref.shape[1]
    scale = 1.0 / (1.0 + jnp.sum(total[width:], axis=0, keepdims=True))
    scale = jnp.broadcast_to(scale, (TILE, TILE)).T
    spans = [slice(c * TILE, (c + 1) * TILE) for c in range(width // TILE)]
    mean = jnp.concatenate([total[span] * scale for span in spans], axis=1).astype(jnp.bfloat16)
    hidden = hidden_ref[...] + jnp.dot(
        mean, w_neigh_ref[...], preferred_element_type=jnp.float32
    )
    active = jnp.maximum(hidden, 0.0)
    out = active * lax.rsqrt(jnp.mean(active * active, axis=-1, keepdims=True) + 1e-05)
    out_ref[...] = out.astype(out_ref.dtype)


def finish(hidden, total, other, w_neigh):
    return pl.pallas_call(
        finish_kernel,
        out_shape=jax.ShapeDtypeStruct(hidden.shape, jnp.bfloat16),
        compiler_params=pltpu.CompilerParams(vmem_limit_bytes=4 << 20),
        name="finish",
    )(hidden, total, other, w_neigh)


def refresh(stale, w_self, w_neigh, tile_weights, tile_pos, tile_counts):
    meta = jnp.stack([lax.axis_index("blk"), lax.axis_index("rep")]).astype(jnp.int32)
    places = jnp.transpose(tile_pos, (0, 3, 1, 2))[0]
    mate = from_other_core(stale)
    single = from_single(stale)
    own_pair = jnp.concatenate([stale, mate], axis=0)
    received = []
    for index in range(3):
        received.append(from_pair(own_pair, index))
    a = place_tiles(meta, tile_counts[0, 0], places, tile_weights[0, 0])
    first, second, third = received
    first, a = lax.optimization_barrier((first, a))
    first_far = from_other_core(first)
    partial = near_sums(0, a, (own_pair, first))
    second, third, single, partial = lax.optimization_barrier((second, third, single, partial))
    second_far = from_other_core(second)
    late_far = from_other_core(jnp.concatenate([third, single], axis=0))
    partial = near_sums(4, a, (second, third), partial)
    args = (meta, a, partial, single, first_far, second_far, late_far)
    both = (0, 1)

    def hop(value, dz, dx=0):
        return to_rep(value, dz, dx)

    own, other = far_sums((4,), both, *args)
    up_other = hop(other, 1)
    down_own = hop(own, -1)
    three_own, three_other, five_own, five_other = far_sums((3, 5), both, *args)
    down_other = hop(five_other, -1)
    up_own = hop(three_own, 1)
    up_other = hop(three_other + up_other, 1)
    down_own = hop(five_own + down_own, -1)
    for slots in ((2, 6), (1, 7)):
        low_own, low_other, high_own, high_other = far_sums(slots, both, *args)
        down_other = hop(high_other + down_other, -1)
        up_own = hop(low_own + up_own, 1)
        up_other = hop(low_other + up_other, 1)
        down_own = hop(high_own + down_own, -1)
    (other,) = far_sums((0,), (1,), *args)
    other = sum(part.astype(jnp.float32) for part in (other, up_other, down_other))
    other = hop(other.astype(jnp.bfloat16), 0, 1)
    (own,) = far_sums((0,), (0,), *args)
    hidden, total = prepare(stale, w_self, own, up_own, down_own)
    return finish(hidden, total, other, w_neigh)


def solution(mesh):
    return jax.shard_map(
        refresh,
        mesh=mesh,
        in_specs=(
            P(("blk", "rep"), None),
            P(),
            P(),
            P("blk", "rep", None, None, None, None),
            P("blk", "rep", None, None),
            P("blk", "rep", None),
        ),
        out_specs=P(("blk", "rep"), None),
        check_vma=False,
    )
```
